32 devices in a mesh: gx: 8 (over z, y), gy: 4 (over x, core).
Axes of the slice: x: 2, y: 2, z: 4, core: 2. Of those that a mesh axis runs over, the one named last changes fastest.
Arguments:
- vorticity_grid: float32 [4096, 4096], P(('gx', 'gy')), may hold values from -6 to 6
- forcing_grid: float32 [4096, 4096], P(('gx', 'gy')), may hold values from -12 to 12
- cutoff: int32 [1], replicated, may hold values from 853 to 1365
- forcing_shells: int32 [4], replicated, may hold values from 2 to 127
Outputs:
- lifted_spectrum: float32 [2, 4096, 4096], P(None, ('gx', 'gy'))
- coarse_field: float32 [256, 256], P(('gx', 'gy'))
The draws below stay inside these ranges and needn't reach their ends.
Inputs may be any that keep to these rules, and one draw needn't show every extreme that they name: Nonlinear modes with an absolute wavenumber index above cutoff are removed.
All inputs are finite; a program needn't handle non-finite values.
Results may differ from the reference program's by a relative error of at most 0.0001.
Values sent between devices are 32-bit elements; how exact they have to be, the bound alone decides.
A program may use at most 128 MiB of HBM per device.

```python
import math
import jax
import jax.numpy as jnp

GRID = 4096
STEPS = 1
LOW = 256
SHELLS = 4


def with_ends(array, rng, least, high):
    longest = array.shape.index(max(array.shape))
    spots = []
    for shift in (0, 1):
        where = [jax.random.randint(jax.random.fold_in(rng, axis), (), 0, length) for axis, length in enumerate(array.shape)]
        where[longest] = (where[longest] + shift) % array.shape[longest]
        spots.append(tuple(where))
    return array.at[spots[0]].set(least).at[spots[1]].set(high)


def levels(rng, shape, shards, least, high):
    loudness, own = 1.0, jax.random.fold_in(rng, 6)
    for position, shards_of in shards:
        steps = jnp.exp(jax.random.uniform(jax.random.fold_in(own, position), (shards_of,), jnp.float32, least / len(shards), high / len(shards)))
        loudness = loudness * jnp.repeat(steps, shape[position] // shards_of).reshape([-1 if axis == position else 1 for axis in range(len(shape))])
    return loudness


def centred(rng, shape, deviation, reach, cuts=(), kind=jnp.bfloat16):
    factor_of = levels(rng, shape, cuts, -0.22, 0.18) if cuts else 1.0
    values = jax.random.normal(rng, shape, jnp.float32) * deviation * factor_of
    return jnp.minimum(jnp.maximum(values, -reach), reach).astype(kind)


def setup_inputs(seed: int = 0) -> dict:
    keys = jax.random.split(jax.random.key(seed), 5)
    vorticity_grid = centred(keys[0], (GRID, GRID), 1.0, 6.0, ((0, 32),), jnp.float32)
    forcing_grid = centred(keys[1], (GRID, GRID), 2.0, 12.0, ((0, 32),), jnp.float32)
    cutoff = jax.random.randint(keys[2], (1,), GRID // 3 - GRID // 8, GRID // 3 + 1).astype(jnp.int32)
    forcing_shells = with_ends(jax.random.randint(keys[3], (SHELLS,), 2, LOW // 2), jax.random.fold_in(keys[3], 1), 2, (LOW // 2) - 1).astype(jnp.int32)
    return dict(vorticity_grid=vorticity_grid, forcing_grid=forcing_grid, cutoff=cutoff, forcing_shells=forcing_shells)


time_step = 0.05
viscosity = 0.05
coarse_ratio = 4.0


def signed_index(index_array, length_of):
    return jnp.where(index_array < length_of // 2, index_array, index_array - length_of)


def to_spectrum(physical):
    return jnp.fft.fft2(physical, norm="ortho").T


def to_grid(spectrum):
    return jnp.fft.ifft2(spectrum.T, norm="ortho")


def reference(vorticity_grid, forcing_grid, cutoff, forcing_shells):
    indices = jnp.arange(GRID, dtype=jnp.int32)
    wave_y = signed_index(indices, GRID)[:, None]
    wave_x = signed_index(indices, GRID)[None, :]
    wave_unit = 2.0 * math.pi / GRID
    deriv_y = jnp.where(indices[:, None] == GRID // 2, 0, wave_y).astype(jnp.float32) * wave_unit
    deriv_x = jnp.where(indices[None, :] == GRID // 2, 0, wave_x).astype(jnp.float32) * wave_unit
    squares = wave_x * wave_x + wave_y * wave_y
    laplace = squares.astype(jnp.float32) * (wave_unit * wave_unit)
    inverse_lap = jnp.where(squares == 0, 0.0, 1.0 / jnp.maximum(laplace, wave_unit * wave_unit))
    dealias = (jnp.abs(wave_x) <= cutoff[0]) & (jnp.abs(wave_y) <= cutoff[0])
    shell_mask = jnp.zeros((GRID, GRID), dtype=bool)
    for shell_index in range(SHELLS):
        radius = forcing_shells[shell_index]
        shell_mask = shell_mask | ((radius * radius <= squares) & (squares < (radius + 1) * (radius + 1)))
    drive = jnp.where(shell_mask, to_spectrum(forcing_grid), 0.0)
    vorticity = to_spectrum(vorticity_grid)

    def tendency(state):
        stream = state * inverse_lap
        velocity_u = to_grid(1j * deriv_y * stream).real
        velocity_v = to_grid(-1j * deriv_x * stream).real
        grad_x = to_grid(1j * deriv_x * state).real
        grad_y = to_grid(1j * deriv_y * state).real
        advect = velocity_u * grad_x + velocity_v * grad_y
        nonlinear = jnp.where(dealias, to_spectrum(advect), 0.0)
        return -nonlinear - viscosity * laplace * state + drive

    earlier = vorticity
    for step_index in range(STEPS):
        earlier = vorticity
        first_slope = tendency(vorticity)
        second_slope = tendency(vorticity + time_step * first_slope)
        vorticity = vorticity + 0.5 * time_step * (first_slope + second_slope)
    projected = vorticity + coarse_ratio * (vorticity - earlier)
    half_low = LOW // 2
    low_modes = (wave_x >= -half_low) & (wave_x < half_low) & (wave_y >= -half_low) & (wave_y < half_low)
    lifted = jnp.where(low_modes, projected, vorticity)
    block_rows = jnp.concatenate([projected[:half_low], projected[GRID - half_low:]], axis=0)
    block_low = jnp.concatenate([block_rows[:, :half_low], block_rows[:, GRID - half_low:]], axis=1)
    coarse = jnp.fft.ifft2(block_low.T, norm="ortho").real
    return jnp.stack([lifted.real, lifted.imag]), coarse
```

```python
import math

import jax
import jax.numpy as jnp
import numpy as np
from jax import lax
from jax.sharding import PartitionSpec as P

LOW = 256
SHELLS = 4
AXES = ("gx", "gy")

time_step = 0.05
viscosity = 0.05
coarse_ratio = 4.0


def contract(pattern, left_side, right_side):
    return jnp.einsum(pattern, left_side, right_side, precision=lax.Precision.HIGH)


def turn(product, length_of):
    phases = 2.0 * np.pi / length_of * (product % length_of)
    return np.cos(phases), np.sin(phases)


def rotation(cos_part, sin_part, axes):
    pairs = np.stack([np.stack([cos_part, -sin_part]), np.stack([sin_part, cos_part])])
    return np.moveaxis(pairs, (0, 1), axes).astype(np.float32)


def wave_tables(grid, total, rows):
    A = max(64, total)
    B = grid // A
    half = B // 2
    scale = 1.0 / math.sqrt(grid)
    k, a = np.arange(A), np.arange(A)
    b, j = np.arange(B), np.arange(half)
    out = {"A": A, "B": B, "half": half}
    cos_t, sin_t = turn(k[:, None] * a[None, :], A)
    out["y1"] = np.stack([cos_t, -sin_t], 1).astype(np.float32)
    ky = k[:, None] + A * j[None, :]
    cos_t, sin_t = turn(ky[:, :, None] * b, grid)
    y2 = rotation(cos_t * scale, -sin_t * scale, (1, 3))
    plain = y2.copy()
    y2[0, 1, 0, 0, :] = scale * (-1.0) ** b
    y2[0, 1, 0, 1, :] = 0.0
    out["y2"], out["y2_plain"] = y2, plain
    weight = np.where(ky == 0, 1.0, 2.0)[:, :, None] * scale
    cos_t, sin_t, weight = (t.swapaxes(1, 2) for t in (cos_t, sin_t, weight))
    iy = rotation(cos_t * weight, sin_t * weight, (1, 3))
    slope = (ky * (2.0 * np.pi / grid))[:, None, :] * weight
    iyd = rotation(-sin_t * slope, cos_t * slope, (1, 3))
    iy[0, 0, :, 1, 0] = scale * (-1.0) ** b
    iy[0, 1, :, 1, 0] = 0.0
    out["iy"], out["iyd"] = iy, iyd
    cos_t, sin_t = turn(a[:, None] * k[None, :], A)
    out["iy1"] = np.stack([cos_t, -sin_t], 2).astype(np.float32)
    p, s = np.arange(total), np.arange(total)
    q, lane = np.arange(rows), np.arange(rows)
    cos_t, sin_t = turn(p[:, None] * s[None, :], total)
    out["x1"] = rotation(cos_t * scale, -sin_t * scale, (1, 3))
    out["ix1"] = rotation(cos_t.T * scale, sin_t.T * scale, (1, 3))
    cos_t, sin_t = turn(q[:, None] * lane[None, :], rows)
    out["x2"] = rotation(cos_t.T, -sin_t.T, (2, 0))
    out["ix2"] = rotation(cos_t, sin_t, (2, 0))
    cos_t, sin_t = turn(p[:, None] * lane[None, :], grid)
    out["tw"] = np.stack([cos_t, sin_t]).astype(np.float32)
    return out


def body(vorticity_grid, forcing_grid, cutoff, forcing_shells):
    rows, grid = vorticity_grid.shape
    total = lax.axis_size("gx") * lax.axis_size("gy")
    rank = lax.axis_index("gx") * lax.axis_size("gy") + lax.axis_index("gy")
    tables = wave_tables(grid, total, rows)
    A, B, half = tables["A"], tables["B"], tables["half"]
    local = A // total
    half_low = LOW // 2
    kept = (grid // 3) // A + 1
    driven = -(-half_low // A)
    unit = 2.0 * math.pi / grid

    def exchange(values):
        return lax.all_to_all(values, AXES, split_axis=0, concat_axis=0, tiled=True)

    def forward_y(fields, table):
        first = contract("kda,abx->kdbx", tables["y1"], fields)
        second = contract("kdjcb,kcbx->kdjx", table, first)
        return second.reshape((total, local) + second.shape[1:])

    def inverse_y(waves, table):
        waves = waves.reshape((A,) + waves.shape[2:])
        first = contract("kdbcj,kcjx->kdbx", table[..., : waves.shape[2]], waves)
        return contract("akd,kdbx->abx", tables["iy1"], first)

    def twiddle(values, direction):
        cos_t = tables["tw"][0][:, None, None, :]
        sin_t = direction * tables["tw"][1][:, None, None, :]
        real, imag = values[:, :, 0], values[:, :, 1]
        return jnp.stack([real * cos_t - imag * sin_t, real * sin_t + imag * cos_t], 2)

    def forward_x(waves):
        first = contract("pdsc,skcjl->pkdjl", tables["x1"], waves)
        return contract("pkcjl,cldq->pkdjq", twiddle(first, -1.0), tables["x2"])

    def inverse_x(waves):
        first = contract("pkcjq,cqdl->pkdjl", waves, tables["ix2"])
        return contract("sdpc,pkcjl->skdjl", tables["ix1"], twiddle(first, 1.0))

    p_ids = jnp.arange(total, dtype=jnp.int32)[:, None, None, None]
    q_ids = jnp.arange(rows, dtype=jnp.int32)[None, None, None, :]
    k_ids = (rank * local + jnp.arange(local, dtype=jnp.int32))[None, :, None, None]
    j_ids = jnp.arange(half, dtype=jnp.int32)[None, None, :, None]
    kx_ids = p_ids + total * q_ids
    wave_x = jnp.where(kx_ids < grid // 2, kx_ids, kx_ids - grid)
    deriv_x = jnp.where(kx_ids == grid // 2, 0, wave_x).astype(jnp.float32) * unit
    wave_y = k_ids + A * j_ids
    nyquist_y = jnp.full((1, 1, 1, 1), -(grid // 2), jnp.int32)
    origin = (k_ids == 0) & (j_ids == 0)

    def laplacian(rows_y):
        return (wave_x * wave_x + rows_y * rows_y).astype(jnp.float32) * (unit * unit)

    def inverse_laplacian(rows_y):
        squares = wave_x * wave_x + rows_y * rows_y
        lap = squares.astype(jnp.float32) * (unit * unit)
        return jnp.where(squares == 0, 0.0, 1.0 / jnp.maximum(lap, unit * unit))

    def slope_x(pair):
        return (-deriv_x * pair[1], deriv_x * pair[0])

    def packed(main, extra):
        real, imag = main
        if extra is not None:
            real = jnp.where(origin, real - extra[1], real)
            imag = jnp.where(origin, imag + extra[0], imag)
        return jnp.stack([real, imag], 2)

    turned = vorticity_grid.T.reshape(A, B, rows)
    start_half = forward_y(turned, tables["y2"])
    force_half = forward_y(
        forcing_grid.T.reshape(A, B, rows), tables["y2_plain"][:, :, :driven]
    )
    moved = exchange(jnp.concatenate([start_half, force_half], 3))
    spectra = forward_x(moved)
    state = (spectra[:, :, 0, :half], spectra[:, :, 1, :half])
    squares = (wave_x * wave_x + wave_y * wave_y)[:, :, :driven]
    shell = jnp.zeros(squares.shape, bool)
    for index in range(SHELLS):
        radius = forcing_shells[index]
        shell = shell | ((radius * radius <= squares) & (squares < (radius + 1) * (radius + 1)))
    drive = tuple(jnp.where(shell, spectra[:, :, c, half:], 0.0) for c in (0, 1))

    def mirrored(natural):
        return jnp.roll(jnp.flip(natural, -1), 1, -1)

    zero_real, zero_imag = state[0][:, 0, 0].T.reshape(grid), state[1][:, 0, 0].T.reshape(grid)
    back_real, back_imag = mirrored(zero_real), -mirrored(zero_imag)
    own_real, own_imag = 0.5 * (zero_real + back_real), 0.5 * (zero_imag + back_imag)
    nyq_real, nyq_imag = 0.5 * (zero_imag - back_imag), -0.5 * (zero_real - back_real)

    def laid(natural):
        return natural.reshape(rows, total).T[:, None, None, :]

    state = tuple(
        jnp.where(origin, laid(own), part) for own, part in zip((own_real, own_imag), state)
    )
    extra = (laid(nyq_real), laid(nyq_imag))
    lap, inv_lap = laplacian(wave_y), inverse_laplacian(wave_y)
    lap_n, inv_lap_n = laplacian(nyquist_y), inverse_laplacian(nyquist_y)
    dealias = ((jnp.abs(wave_x) <= cutoff[0]) & (jnp.abs(wave_y) <= cutoff[0]))[:, :, :kept]

    def widened(part, count):
        return jnp.pad(part, ((0, 0), (0, 0), (0, count - part.shape[2]), (0, 0)))

    drive_kept = tuple(widened(part, kept) for part in drive)

    def product(psi, psi_x, vort, vort_x):
        speed_u = inverse_y(psi, tables["iyd"])
        slope_wx = inverse_y(vort_x, tables["iy"])
        speed_v = -inverse_y(psi_x, tables["iy"])
        slope_wy = inverse_y(vort, tables["iyd"])
        advect = speed_u * slope_wx + speed_v * slope_wy
        term = forward_x(exchange(forward_y(advect, tables["y2_plain"][:, :, :kept])))
        return tuple(
            drive_kept[c] - jnp.where(dealias, term[:, :, c], 0.0) for c in (0, 1)
        )

    psi = tuple(inv_lap * part for part in state)
    psi_extra = tuple(inv_lap_n * part for part in extra)
    outgoing = jnp.concatenate(
        [
            packed(psi, psi_extra),
            packed(slope_x(psi), slope_x(psi_extra)),
            packed(slope_x(state), slope_x(extra)),
        ],
        3,
    )
    arrived = exchange(inverse_x(outgoing))
    psi_half = arrived[:, :, :, :half]
    psi_x_half = arrived[:, :, :, half : 2 * half]
    vort_x_half = arrived[:, :, :, 2 * half :]
    first = product(psi_half, psi_x_half, start_half, vort_x_half)

    moved_on = tuple(
        part - time_step * viscosity * lap * part + time_step * widened(term, half)
        for part, term in zip(state, first)
    )
    moved_extra = tuple(part - time_step * viscosity * lap_n * part for part in extra)
    psi_kept = tuple(time_step * inv_lap[:, :, :kept] * term for term in first)
    outgoing = jnp.concatenate(
        [
            packed(moved_on, moved_extra),
            packed(slope_x(moved_on), slope_x(moved_extra)),
            jnp.stack(psi_kept, 2),
            jnp.stack(slope_x(psi_kept), 2),
        ],
        3,
    )
    arrived = exchange(inverse_x(outgoing))

    def added(whole, local_part, part):
        part = jnp.pad(part, ((0, 0), (0, 0), (0, 0), (0, half - kept), (0, 0)))
        return whole - time_step * viscosity * local_part + part

    second = product(
        added(psi_half, start_half, arrived[:, :, :, 2 * half : 2 * half + kept]),
        added(psi_x_half, vort_x_half, arrived[:, :, :, 2 * half + kept :]),
        arrived[:, :, :, :half],
        arrived[:, :, :, half : 2 * half],
    )

    def stepped(part, ahead, lap_of, terms):
        linear = -viscosity * lap_of * (part + ahead)
        return part + 0.5 * time_step * (linear if terms is None else linear + terms)

    final = tuple(
        stepped(part, ahead, lap, widened(one + two, half))
        for part, ahead, one, two in zip(state, moved_on, first, second)
    )
    final_extra = tuple(
        stepped(part, ahead, lap_n, None) for part, ahead in zip(extra, moved_extra)
    )
    projected = tuple(new + coarse_ratio * (new - old) for new, old in zip(final, state))

    def lifted(signed_x, signed_y):
        low = (
            (signed_x >= -half_low)
            & (signed_x < half_low)
            & (signed_y >= -half_low)
            & (signed_y < half_low)
        )
        return jnp.stack(
            [jnp.where(low, ahead, now) for ahead, now in zip(projected, final)], 2
        )

    straight = lifted(wave_x, wave_y)
    mirror = lifted(-wave_x, -wave_y)
    nyquist = jnp.stack([part[:, 0] for part in final_extra], 1)[:, None]
    flipped = jnp.flip(mirror, 3)
    shifted = jnp.concatenate(
        [jnp.broadcast_to(nyquist, flipped[:, :, :, :1].shape), flipped[:, :, :, :-1]], 3
    )
    flipped = jnp.where((k_ids == 0)[:, :, None], shifted, flipped)
    whole = jnp.concatenate([straight, flipped], 3)
    sent = whole.transpose(3, 1, 2, 0, 4)
    if rows >= A:
        sent = sent.reshape(total, rows // A, local, 2, total, rows)
        got = exchange(sent)
        sources = got.reshape(total, rows // A, local, 2, total, rows)
        placed = sources.transpose(3, 1, 0, 2, 5, 4).reshape(2, rows, grid)
        back = jnp.roll(
            jnp.flip(placed.reshape(2, rows // A, A, grid), 2), 1, 2
        ).reshape(2, rows, grid)
    else:
        parts = A // rows
        sent = jnp.broadcast_to(sent[:, None], (B, parts) + sent.shape[1:])
        block = exchange(sent.reshape((total,) + sent.shape[2:])).reshape(A, 2, total, rows)
        block = block.transpose(1, 0, 3, 2).reshape(2, A, grid)
        start = (rank % parts) * rows
        placed = lax.dynamic_slice_in_dim(block, start, rows, 1)
        turned_block = jnp.roll(jnp.flip(block, 1), 1, 1)
        back = lax.dynamic_slice_in_dim(turned_block, start, rows, 1)
    back = mirrored(back)
    back = jnp.stack([back[0], -back[1]])
    spectrum = jnp.where(rank >= total // 2, back, placed)

    own = LOW // total
    block_ids = np.arange(LOW)
    col_cos, col_sin = (t.astype(np.float32) / 16.0 for t in turn(block_ids[:, None] * block_ids, LOW))
    low = jnp.concatenate([spectrum[:, :, :half_low], spectrum[:, :, grid - half_low :]], 2)
    column = np.stack([np.stack([col_cos, col_sin]), np.stack([-col_sin, col_cos])])
    mixed = contract("cqp,cdpa->dqa", low, column)
    mixed = mixed.reshape(2, rows, total, own).transpose(2, 0, 1, 3)
    mixed = exchange(mixed)
    count = -(-half_low // rows)
    mixed = jnp.concatenate([mixed[:count], mixed[total - count :]], 0)
    if rows * count != half_low:
        first_rows = mixed[:count].transpose(1, 0, 2, 3).reshape(2, count * rows, own)[:, :half_low]
        last_rows = mixed[count:].transpose(1, 0, 2, 3).reshape(2, count * rows, own)[:, -half_low:]
        mixed = jnp.concatenate([first_rows, last_rows], 1)
    else:
        mixed = mixed.transpose(1, 0, 2, 3).reshape(2, LOW, own)
    row_table = np.stack([col_cos, -col_sin])
    coarse = contract("cqa,cqb->ab", mixed, row_table)
    return (spectrum, coarse)


def solution(mesh):
    placed = (P(AXES, None), P(AXES, None), P(), P())
    return jax.shard_map(
        body,
        mesh=mesh,
        in_specs=placed,
        out_specs=(P(None, AXES, None), P(AXES, None)),
        check_vma=False,
    )
```

```python
import math

import jax
import jax.numpy as jnp
import numpy as np
from jax import lax
from jax.sharding import PartitionSpec as P

LOW = 256
SHELLS = 4
AXES = ("gx", "gy")

time_step = 0.05
viscosity = 0.05
coarse_ratio = 4.0


def contract(pattern, left_side, right_side):
    return jnp.einsum(pattern, left_side, right_side, precision=lax.Precision.HIGH)


def turn(product, length_of):
    phases = 2.0 * np.pi / length_of * (product % length_of)
    return np.cos(phases), np.sin(phases)


def rotation(cos_part, sin_part, axes):
    pairs = np.stack([np.stack([cos_part, -sin_part]), np.stack([sin_part, cos_part])])
    return np.moveaxis(pairs, (0, 1), axes).astype(np.float32)


def wave_tables(grid, total, rows):
    A = max(64, total)
    B = grid // A
    half = B // 2
    scale = 1.0 / math.sqrt(grid)
    k, a = np.arange(A), np.arange(A)
    b, j = np.arange(B), np.arange(half)
    out = {"A": A, "B": B, "half": half}
    cos_t, sin_t = turn(k[:, None] * a[None, :], A)
    out["y1"] = np.stack([cos_t, -sin_t], 1).astype(np.float32)
    out["kb"] = np.stack(turn(k[:, None] * b[None, :], grid)).astype(np.float32)
    out["jb"] = np.stack(turn(j[:, None] * b[None, :], B)).astype(np.float32)
    cos_t, sin_t = turn(a[:, None] * k[None, :], A)
    out["iy1"] = np.stack([cos_t, -sin_t], 2).astype(np.float32)
    p, s = np.arange(total), np.arange(total)
    q, lane = np.arange(rows), np.arange(rows)
    cos_t, sin_t = turn(p[:, None] * s[None, :], total)
    out["x1"] = rotation(cos_t * scale, -sin_t * scale, (1, 3))
    out["ix1"] = rotation(cos_t.T * scale, sin_t.T * scale, (1, 3))
    cos_t, sin_t = turn(q[:, None] * lane[None, :], rows)
    out["x2"] = rotation(cos_t.T, -sin_t.T, (2, 0))
    out["ix2"] = rotation(cos_t, sin_t, (2, 0))
    cos_t, sin_t = turn(p[:, None] * lane[None, :], grid)
    out["tw"] = np.stack([cos_t, sin_t]).astype(np.float32)
    return out


def second_tables(tables, grid):
    scale = 1.0 / math.sqrt(grid)
    kb, jb = lax.optimization_barrier((tables["kb"], tables["jb"]))
    k = lax.broadcasted_iota(jnp.int32, (tables["A"], 1, 1, 1, 1), 0)

    def multiplied(left, right):
        return (left[0] * right[0] - left[1] * right[1], left[1] * right[0] + left[0] * right[1])

    def paired(cos_part, sin_part):
        to_real = jnp.stack([cos_part, -sin_part], 2)
        to_imag = jnp.stack([sin_part, cos_part], 2)
        return jnp.stack([to_real, to_imag], 1)

    half, width = tables["half"], tables["B"]
    sign = scale * (1.0 - 2.0 * (lax.iota(jnp.int32, width) % 2).astype(jnp.float32))
    d = lax.broadcasted_iota(jnp.int32, (1, 2, 1, 1, 1), 1)
    cos_t, sin_t = multiplied(kb[:, :, None, :], jb[:, None, :, :])
    plain = paired(scale * cos_t, -scale * sin_t)
    j = lax.broadcasted_iota(jnp.int32, (1, 1, half, 1, 1), 2)
    c = lax.broadcasted_iota(jnp.int32, (1, 1, 1, 2, 1), 3)
    riding = jnp.where(c == 0, sign[None, None, None, None, :], 0.0)
    table = jnp.where((k == 0) & (d == 1) & (j == 0), riding, plain)
    cos_t, sin_t = multiplied(kb[:, :, :, None], jb.swapaxes(1, 2)[:, None])
    ky = k[:, :, :, 0, 0] + tables["A"] * lax.broadcasted_iota(jnp.int32, (1, 1, half), 2)
    weight = jnp.where(ky == 0, scale, 2.0 * scale)
    slope = ky.astype(jnp.float32) * (2.0 * math.pi / grid) * weight
    back = paired(cos_t * weight, sin_t * weight)
    j = lax.broadcasted_iota(jnp.int32, (1, 1, 1, 1, half), 4)
    riding = jnp.where(d == 0, sign[None, None, :, None, None], 0.0)
    back = jnp.where((k == 0) & (c == 1) & (j == 0), riding, back)
    back_slope = paired(-sin_t * slope, cos_t * slope)
    return {"y2": table, "y2_plain": plain, "iy": back, "iyd": back_slope}


def body(vorticity_grid, forcing_grid, cutoff, forcing_shells):
    rows, grid = vorticity_grid.shape
    total = lax.axis_size("gx") * lax.axis_size("gy")
    rank = lax.axis_index("gx") * lax.axis_size("gy") + lax.axis_index("gy")
    tables = wave_tables(grid, total, rows)
    tables.update(second_tables(tables, grid))
    A, B, half = tables["A"], tables["B"], tables["half"]
    local = A // total
    half_low = LOW // 2
    kept = (grid // 3) // A + 1
    driven = -(-half_low // A)
    unit = 2.0 * math.pi / grid

    def exchange(values):
        return lax.all_to_all(values, AXES, split_axis=0, concat_axis=0, tiled=True)

    def forward_y(fields, table):
        first = contract("kda,abx->kdbx", tables["y1"], fields)
        second = contract("kdjcb,kcbx->kdjx", table, first)
        return second.reshape((total, local) + second.shape[1:])

    def inverse_y(waves, table):
        waves = waves.reshape((A,) + waves.shape[2:])
        first = contract("kdbcj,kcjx->kdbx", table[..., : waves.shape[2]], waves)
        return contract("akd,kdbx->abx", tables["iy1"], first)

    def twiddle(values, direction):
        cos_t = tables["tw"][0][:, None, None, :]
        sin_t = direction * tables["tw"][1][:, None, None, :]
        real, imag = values[:, :, 0], values[:, :, 1]
        return jnp.stack([real * cos_t - imag * sin_t, real * sin_t + imag * cos_t], 2)

    def forward_x(waves):
        first = contract("pdsc,skcjl->pkdjl", tables["x1"], waves)
        return contract("pkcjl,cldq->pkdjq", twiddle(first, -1.0), tables["x2"])

    def inverse_x(waves):
        first = contract("pkcjq,cqdl->pkdjl", waves, tables["ix2"])
        return contract("sdpc,pkcjl->skdjl", tables["ix1"], twiddle(first, 1.0))

    p_ids = jnp.arange(total, dtype=jnp.int32)[:, None, None, None]
    q_ids = jnp.arange(rows, dtype=jnp.int32)[None, None, None, :]
    k_ids = (rank * local + jnp.arange(local, dtype=jnp.int32))[None, :, None, None]
    j_ids = jnp.arange(half, dtype=jnp.int32)[None, None, :, None]
    kx_ids = p_ids + total * q_ids
    wave_x = jnp.where(kx_ids < grid // 2, kx_ids, kx_ids - grid)
    deriv_x = jnp.where(kx_ids == grid // 2, 0, wave_x).astype(jnp.float32) * unit
    wave_y = k_ids + A * j_ids
    nyquist_y = jnp.full((1, 1, 1, 1), -(grid // 2), jnp.int32)
    origin = (k_ids == 0) & (j_ids == 0)

    def laplacian(rows_y):
        return (wave_x * wave_x + rows_y * rows_y).astype(jnp.float32) * (unit * unit)

    def inverse_laplacian(rows_y):
        squares = wave_x * wave_x + rows_y * rows_y
        lap = squares.astype(jnp.float32) * (unit * unit)
        return jnp.where(squares == 0, 0.0, 1.0 / jnp.maximum(lap, unit * unit))

    def slope_x(pair):
        return (-deriv_x * pair[1], deriv_x * pair[0])

    def packed(main, extra):
        real, imag = main
        if extra is not None:
            real = jnp.where(origin, real - extra[1], real)
            imag = jnp.where(origin, imag + extra[0], imag)
        return jnp.stack([real, imag], 2)

    turned = vorticity_grid.T.reshape(A, B, rows)
    start_half = forward_y(turned, tables["y2"])
    force_half = forward_y(
        forcing_grid.T.reshape(A, B, rows), tables["y2_plain"][:, :, :driven]
    )
    moved = exchange(jnp.concatenate([start_half, force_half], 3))
    spectra = forward_x(moved)
    state = (spectra[:, :, 0, :half], spectra[:, :, 1, :half])
    squares = (wave_x * wave_x + wave_y * wave_y)[:, :, :driven]
    shell = jnp.zeros(squares.shape, bool)
    for index in range(SHELLS):
        radius = forcing_shells[index]
        shell = shell | ((radius * radius <= squares) & (squares < (radius + 1) * (radius + 1)))
    drive = tuple(jnp.where(shell, spectra[:, :, c, half:], 0.0) for c in (0, 1))

    def mirrored(natural):
        return jnp.roll(jnp.flip(natural, -1), 1, -1)

    zero_real, zero_imag = state[0][:, 0, 0].T.reshape(grid), state[1][:, 0, 0].T.reshape(grid)
    back_real, back_imag = mirrored(zero_real), -mirrored(zero_imag)
    own_real, own_imag = 0.5 * (zero_real + back_real), 0.5 * (zero_imag + back_imag)
    nyq_real, nyq_imag = 0.5 * (zero_imag - back_imag), -0.5 * (zero_real - back_real)

    def laid(natural):
        return natural.reshape(rows, total).T[:, None, None, :]

    state = tuple(
        jnp.where(origin, laid(own), part) for own, part in zip((own_real, own_imag), state)
    )
    extra = (laid(nyq_real), laid(nyq_imag))
    lap, inv_lap = laplacian(wave_y), inverse_laplacian(wave_y)
    lap_n, inv_lap_n = laplacian(nyquist_y), inverse_laplacian(nyquist_y)
    dealias = ((jnp.abs(wave_x) <= cutoff[0]) & (jnp.abs(wave_y) <= cutoff[0]))[:, :, :kept]

    def widened(part, count):
        return jnp.pad(part, ((0, 0), (0, 0), (0, count - part.shape[2]), (0, 0)))

    drive_kept = tuple(widened(part, kept) for part in drive)

    def product(psi, psi_x, vort, vort_x):
        speed_u = inverse_y(psi, tables["iyd"])
        slope_wx = inverse_y(vort_x, tables["iy"])
        speed_v = -inverse_y(psi_x, tables["iy"])
        slope_wy = inverse_y(vort, tables["iyd"])
        advect = speed_u * slope_wx + speed_v * slope_wy
        term = forward_x(exchange(forward_y(advect, tables["y2_plain"][:, :, :kept])))
        return tuple(
            drive_kept[c] - jnp.where(dealias, term[:, :, c], 0.0) for c in (0, 1)
        )

    psi = tuple(inv_lap * part for part in state)
    psi_extra = tuple(inv_lap_n * part for part in extra)
    outgoing = jnp.concatenate(
        [
            packed(psi, psi_extra),
            packed(slope_x(psi), slope_x(psi_extra)),
            packed(slope_x(state), slope_x(extra)),
        ],
        3,
    )
    arrived = exchange(inverse_x(outgoing))
    psi_half = arrived[:, :, :, :half]
    psi_x_half = arrived[:, :, :, half : 2 * half]
    vort_x_half = arrived[:, :, :, 2 * half :]
    first = product(psi_half, psi_x_half, start_half, vort_x_half)

    moved_on = tuple(
        part - time_step * viscosity * lap * part + time_step * widened(term, half)
        for part, term in zip(state, first)
    )
    moved_extra = tuple(part - time_step * viscosity * lap_n * part for part in extra)
    psi_kept = tuple(time_step * inv_lap[:, :, :kept] * term for term in first)
    outgoing = jnp.concatenate(
        [
            packed(moved_on, moved_extra),
            packed(slope_x(moved_on), slope_x(moved_extra)),
            jnp.stack(psi_kept, 2),
            jnp.stack(slope_x(psi_kept), 2),
        ],
        3,
    )
    arrived = exchange(inverse_x(outgoing))

    def added(whole, local_part, part):
        part = jnp.pad(part, ((0, 0), (0, 0), (0, 0), (0, half - kept), (0, 0)))
        return whole - time_step * viscosity * local_part + part

    second = product(
        added(psi_half, start_half, arrived[:, :, :, 2 * half : 2 * half + kept]),
        added(psi_x_half, vort_x_half, arrived[:, :, :, 2 * half + kept :]),
        arrived[:, :, :, :half],
        arrived[:, :, :, half : 2 * half],
    )

    def stepped(part, ahead, lap_of, terms):
        linear = -viscosity * lap_of * (part + ahead)
        return part + 0.5 * time_step * (linear if terms is None else linear + terms)

    final = tuple(
        stepped(part, ahead, lap, widened(one + two, half))
        for part, ahead, one, two in zip(state, moved_on, first, second)
    )
    final_extra = tuple(
        stepped(part, ahead, lap_n, None) for part, ahead in zip(extra, moved_extra)
    )
    projected = tuple(new + coarse_ratio * (new - old) for new, old in zip(final, state))

    def lifted(signed_x, signed_y):
        low = (
            (signed_x >= -half_low)
            & (signed_x < half_low)
            & (signed_y >= -half_low)
            & (signed_y < half_low)
        )
        return jnp.stack(
            [jnp.where(low, ahead, now) for ahead, now in zip(projected, final)], 2
        )

    straight = lifted(wave_x, wave_y)
    mirror = lifted(-wave_x, -wave_y)
    nyquist = jnp.stack([part[:, 0] for part in final_extra], 1)[:, None]
    flipped = jnp.flip(mirror, 3)
    shifted = jnp.concatenate(
        [jnp.broadcast_to(nyquist, flipped[:, :, :, :1].shape), flipped[:, :, :, :-1]], 3
    )
    flipped = jnp.where((k_ids == 0)[:, :, None], shifted, flipped)
    lanes = np.arange(rows)
    head_turn = (lanes[:, None] == (rows - lanes[None, :]) % rows).astype(np.float32)
    tail_turn = (lanes[:, None] == rows - 1 - lanes[None, :]).astype(np.float32)
    flipped = flipped * jnp.array([1.0, -1.0], jnp.float32)[None, None, :, None, None]
    highest = lax.Precision.HIGHEST
    head = jnp.einsum("pkdjq,qr->pkdjr", flipped[:1], head_turn, precision=highest)
    tail = jnp.einsum("pkdjq,qr->pkdjr", flipped[1:], tail_turn, precision=highest)
    flipped = jnp.concatenate([head, jnp.flip(tail, 0)], 0)
    whole = jnp.concatenate([straight, flipped], 3)
    backwards = rank >= total // 2
    if rows >= A:
        shape = (total, local, 2, total, rows // A, rows)
        sent = whole.reshape(shape).transpose(3, 1, 4, 2, 0, 5)
        block = exchange(sent).reshape(A, rows // A, 2, total, rows)
        block = jnp.where(backwards, jnp.roll(jnp.flip(block, 0), 1, 0), block)
        spectrum = block.transpose(2, 1, 0, 4, 3).reshape(2, rows, grid)
    else:
        parts = A // rows
        sent = whole.transpose(3, 1, 2, 0, 4)
        sent = jnp.broadcast_to(sent[:, None], (B, parts) + sent.shape[1:])
        block = exchange(sent.reshape((total,) + sent.shape[2:])).reshape(A, 2, total, rows)
        block = jnp.where(backwards, jnp.roll(jnp.flip(block, 0), 1, 0), block)
        block = lax.dynamic_slice_in_dim(block, (rank % parts) * rows, rows, 0)
        spectrum = block.transpose(1, 0, 3, 2).reshape(2, rows, grid)

    own = LOW // total
    block_ids = np.arange(LOW)
    col_cos, col_sin = (t.astype(np.float32) / 16.0 for t in turn(block_ids[:, None] * block_ids, LOW))
    low = jnp.concatenate([spectrum[:, :, :half_low], spectrum[:, :, grid - half_low :]], 2)
    column = np.stack([np.stack([col_cos, col_sin]), np.stack([-col_sin, col_cos])])
    mixed = contract("cqp,cdpa->dqa", low, column)
    mixed = mixed.reshape(2, rows, total, own).transpose(2, 0, 1, 3)
    mixed = exchange(mixed)
    count = -(-half_low // rows)
    mixed = jnp.concatenate([mixed[:count], mixed[total - count :]], 0)
    if rows * count != half_low:
        first_rows = mixed[:count].transpose(1, 0, 2, 3).reshape(2, count * rows, own)[:, :half_low]
        last_rows = mixed[count:].transpose(1, 0, 2, 3).reshape(2, count * rows, own)[:, -half_low:]
        mixed = jnp.concatenate([first_rows, last_rows], 1)
    else:
        mixed = mixed.transpose(1, 0, 2, 3).reshape(2, LOW, own)
    row_table = np.stack([col_cos, -col_sin])
    coarse = contract("cqa,cqb->ab", mixed, row_table)
    return (spectrum, coarse)


def solution(mesh):
    placed = (P(AXES, None), P(AXES, None), P(), P())
    return jax.shard_map(
        body,
        mesh=mesh,
        in_specs=placed,
        out_specs=(P(None, AXES, None), P(AXES, None)),
        check_vma=False,
    )
```
